32 devices in a mesh: members: 2 (over x), band: 16 (over z, y, core).
Axes of the slice: x: 2, y: 2, z: 4, core: 2. Of those that a mesh axis runs over, the one named last changes fastest.
Arguments:
- grid_inputs: bfloat16 [96, 384, 256], P(('members', 'band')), parts along dimension 0, may hold values from -6 to 6
- stencil_prenorm_scale: float32 [256], replicated, may hold values from 0.1 to 1.9
- patch_kernel_profiles: float32 [48, 9, 27], P('band'), may hold values from -1.2 to 1.2
- channel_mixer_tensor: bfloat16 [2304, 256], replicated, may hold values from -0.125 to 0.125
- softmax_prenorm_scale: float32 [256], replicated, may hold values from 0.1 to 1.9
- probe_lookup_content_projector: bfloat16 [256, 768], replicated, may hold values from -0.375 to 0.375
- head_logit_scales: float32 [8], replicated, may hold values from 3 to 500
- final_projector: bfloat16 [256, 256], replicated, may hold values from -0.375 to 0.375
- azimuth_reaches: int32 [48, 5], P('band'), may hold values from 1 to 8, as said below
Outputs:
- encoded: bfloat16 [96, 384, 256], P(('members', 'band')), parts along dimension 0
The draws below stay inside these ranges and needn't reach their ends.
There are 2 independent parts, one for each index of `members`. The reference program is written for one: setup_inputs(seed, part) draws one part's arguments, and reference() takes and returns one part's arrays. A program takes and returns all parts, laid end to end along the dimension named above; an argument that names none is the same for every part. Nothing has to cross between parts.
Inputs may be any that keep to these rules, and one draw needn't show every extreme that they name: azimuth_reaches[i, a] is the longitude reach of row i's disc in its row at offset a - 2; the rows at the poles reach 8.
All inputs are finite; a program needn't handle non-finite values.
Results may differ from the reference program's by a relative error of at most 0.025.
The reference program's roundings to bfloat16 on the way count: a program that leaves them out, or rounds other values in their place, can miss the bound.
Values may be sent and summed in bfloat16 or wider, within the bound.
No kernel may reach another device: no remote copies, remote signals or barrier semaphores. Data moves between devices by JAX's collectives and lax.ppermute only.
A program may use at most 64 MiB of HBM per device.

```python
import math
import jax
import jax.numpy as jnp
from jax import lax

LONGITUDES = 384
HEAD_COUNT = 8
HEAD_WIDTH = 32
CHANNELS = 256
BASIS_COUNT = 9
CONV_REACH = 4
PATCH_LAT_EXTENT = 2
DISC_REACH = 8
QUERY_BLOCK = 48
LATITUDES = 48


def draw_head_logit_scales(key, part):
    first = jax.random.fold_in(key, 0)
    gentle = jnp.exp(jax.random.uniform(first, (HEAD_COUNT,), jnp.float32, math.log(3.0), math.log(12.0)))
    return gentle


def draw_azimuth_reaches(key, part):
    row_ids = jnp.arange(LATITUDES, dtype=jnp.int32)
    distance = jnp.abs(2 * row_ids - (LATITUDES - 1))
    edge_row = LATITUDES - 1
    base_span = 1 + DISC_REACH * distance * distance // (edge_row * edge_row)
    jitter = jax.random.randint(key, (LATITUDES, 2 * PATCH_LAT_EXTENT + 1), 0, 2, dtype=jnp.int32)
    return jnp.minimum(DISC_REACH, base_span[:, None] + jitter).astype(jnp.int32)


def steps_of(key, dims, cuts, least, top_value):
    factor_of = 1.0
    for axis_at, shards_of in cuts:
        steps = jax.random.uniform(jax.random.fold_in(jax.random.fold_in(key, 6), axis_at), (shards_of,), jnp.float32, least / len(cuts), top_value / len(cuts))
        factor_of = factor_of * jnp.repeat(jnp.exp(steps), dims[axis_at] // shards_of).reshape((-1,) + (1,) * (len(dims) - 1 - axis_at))
    return factor_of


def normal_values(stream_key, dims, scale, limit, cuts=(), held_as=jnp.bfloat16):
    factor_of = steps_of(stream_key, dims, cuts, -0.22, 0.18) if cuts else 1.0
    array = jax.random.normal(stream_key, dims, jnp.float32) * scale * factor_of
    return jnp.minimum(jnp.maximum(array, -limit), limit).astype(held_as)


def setup_inputs(seed: int = 0, part: int = 0) -> dict:
    splits = jax.random.split(jax.random.key(seed), 10)
    own_keys = jax.random.split(jax.random.fold_in(splits[9], part), 10)
    return {
        "grid_inputs": normal_values(own_keys[0], (LATITUDES, LONGITUDES, CHANNELS), 1.0, 6.0, ((0, 16),)),
        "stencil_prenorm_scale": jnp.clip(1.0 + 0.18 * jax.random.normal(splits[1], (CHANNELS,), jnp.float32), 0.1, 1.9),
        "patch_kernel_profiles": normal_values(splits[2], (LATITUDES, BASIS_COUNT, 3 * (2 * CONV_REACH + 1)), 0.2, 1.2, ((0, 16),), jnp.float32),
        "channel_mixer_tensor": normal_values(splits[3], (BASIS_COUNT * CHANNELS, CHANNELS), (BASIS_COUNT * CHANNELS) ** -0.5, 0.125),
        "softmax_prenorm_scale": jnp.clip(1.0 + 0.18 * jax.random.normal(splits[4], (CHANNELS,), jnp.float32), 0.1, 1.9),
        "probe_lookup_content_projector": normal_values(splits[5], (CHANNELS, 3 * CHANNELS), CHANNELS ** -0.5, 0.375),
        "head_logit_scales": draw_head_logit_scales(jax.random.fold_in(splits[9], 71), part),
        "final_projector": normal_values(splits[7], (CHANNELS, CHANNELS), CHANNELS ** -0.5, 0.375),
        "azimuth_reaches": draw_azimuth_reaches(jax.random.fold_in(splits[9], 71), part),
    }


EPSILON = 1e-06

def rms_norm(values, gain_vector):
    values = values.astype(jnp.float32)
    inverse = lax.rsqrt(lax.optimization_barrier(jnp.mean(values * values, axis=-1, keepdims=True)) + EPSILON)
    return values * inverse * gain_vector

def reflect(rim_rows):
    return jnp.roll(jnp.flip(rim_rows, axis=-3), rim_rows.shape[-2] // 2, axis=-2)

def pole_extend(field_rows, rim_width):
    return jnp.concatenate([reflect(field_rows[:rim_width]), field_rows, reflect(field_rows[-rim_width:])], axis=0)

def unit_heads(values):
    shaped = values.astype(jnp.float32).reshape(values.shape[:-1] + (HEAD_COUNT, HEAD_WIDTH))
    inverse = lax.rsqrt(lax.optimization_barrier(jnp.sum(shaped * shaped, axis=-1, keepdims=True)) + EPSILON)
    return (shaped * inverse).reshape(values.shape).astype(jnp.bfloat16)

def conv_filters(patch_kernel_profiles, azimuth_reaches):
    tap_count = 2 * CONV_REACH + 1
    offsets = jnp.abs(jnp.arange(tap_count, dtype=jnp.int32) - CONV_REACH)
    limits = azimuth_reaches[:, PATCH_LAT_EXTENT - 1:PATCH_LAT_EXTENT + 2]
    visible = offsets[None, None, :] <= limits[:, :, None]
    shaped = patch_kernel_profiles.reshape(patch_kernel_profiles.shape[0], BASIS_COUNT, 3, tap_count)
    masked = jnp.where(visible[:, None], shaped, jnp.float32(0.0))
    return masked.astype(jnp.bfloat16).reshape(patch_kernel_profiles.shape)

def lon_taps(window):
    shifted = jnp.stack([jnp.roll(window, CONV_REACH - offset, axis=1) for offset in range(2 * CONV_REACH + 1)], axis=1)
    return shifted.reshape((-1,) + window.shape[1:])

def lon_windows(rim_rows):
    padded = jnp.concatenate([rim_rows[:, -DISC_REACH:], rim_rows, rim_rows[:, :QUERY_BLOCK - DISC_REACH]], axis=1)
    blocks = padded.reshape(padded.shape[0], -1, QUERY_BLOCK, padded.shape[-1])
    windows = jnp.concatenate([blocks[:, :-1], blocks[:, 1:, :2 * DISC_REACH]], axis=2)
    return windows.reshape(windows.shape[:3] + (HEAD_COUNT, HEAD_WIDTH))

def look_at_one_parallel(lone_probe_parallel, lookup_strip_parallels, content_strip_parallels, parallel_azimuth_reach, head_logit_scales):
    window_width = QUERY_BLOCK + 2 * DISC_REACH
    probe_tensor = lone_probe_parallel.astype(jnp.float32).reshape(-1, QUERY_BLOCK, HEAD_COUNT, HEAD_WIDTH)
    lookup_patch_neighbours = lon_windows(lookup_strip_parallels).astype(jnp.float32)
    value_windows = lon_windows(content_strip_parallels).astype(jnp.float32)
    similarity_logits = jnp.einsum('kyge,wknge->kgywn', probe_tensor, lookup_patch_neighbours) * head_logit_scales[None, :, None, None, None]
    positions = jnp.arange(QUERY_BLOCK, dtype=jnp.int32)
    columns = jnp.arange(window_width, dtype=jnp.int32)
    distance = jnp.abs(columns[None, :] - DISC_REACH - positions[:, None])
    visible = distance[:, None, :] <= parallel_azimuth_reach[None, :, None]
    similarity_logits = jnp.where(visible[None, None], similarity_logits, jnp.float32(-1e+30))
    flattened = similarity_logits.reshape(similarity_logits.shape[:3] + (-1,))
    row_peak = lax.optimization_barrier(jnp.max(flattened, axis=-1, keepdims=True))
    exponent = jnp.exp(flattened - row_peak)
    weights = (exponent / lax.optimization_barrier(jnp.sum(exponent, axis=-1, keepdims=True))).astype(jnp.bfloat16).reshape(similarity_logits.shape)
    mixture = jnp.einsum('nhqaw,anwhd->nqhd', weights.astype(jnp.float32), value_windows)
    return mixture.astype(jnp.bfloat16).reshape(LONGITUDES, CHANNELS)

def reference(grid_inputs, stencil_prenorm_scale, patch_kernel_profiles, channel_mixer_tensor, softmax_prenorm_scale, probe_lookup_content_projector, head_logit_scales, final_projector, azimuth_reaches):
    normed = rms_norm(grid_inputs, stencil_prenorm_scale).astype(jnp.bfloat16)
    extended = pole_extend(normed, 1)
    filters = conv_filters(patch_kernel_profiles, azimuth_reaches)

    def conv_row(present_parallel_number):
        window = lax.dynamic_slice_in_dim(extended, present_parallel_number, 3, 0)
        tap_stack = lon_taps(window).astype(jnp.float32)
        basis_sums = jnp.einsum('kt,tjc->jkc', filters[present_parallel_number].astype(jnp.float32), tap_stack).astype(jnp.bfloat16)
        return jnp.dot(basis_sums.reshape(LONGITUDES, -1), channel_mixer_tensor, preferred_element_type=jnp.float32)
    row_ids = jnp.arange(LATITUDES, dtype=jnp.int32)
    hidden = grid_inputs.astype(jnp.float32) + lax.map(conv_row, row_ids)
    attn_in = rms_norm(hidden, softmax_prenorm_scale).astype(jnp.bfloat16)
    projected = jnp.dot(attn_in.reshape(-1, CHANNELS), probe_lookup_content_projector, preferred_element_type=jnp.float32).astype(jnp.bfloat16)
    projected = projected.reshape(LATITUDES, LONGITUDES, 3 * CHANNELS)
    rescaled_probe = unit_heads(projected[..., :CHANNELS])
    lookup_vectors_padded = pole_extend(unit_heads(projected[..., CHANNELS:2 * CHANNELS]), PATCH_LAT_EXTENT)
    content_vectors_padded = pole_extend(projected[..., 2 * CHANNELS:], PATCH_LAT_EXTENT)

    def attend_global(present_parallel_number):
        return look_at_one_parallel(rescaled_probe[present_parallel_number], lax.dynamic_slice_in_dim(lookup_vectors_padded, present_parallel_number, 2 * PATCH_LAT_EXTENT + 1, 0), lax.dynamic_slice_in_dim(content_vectors_padded, present_parallel_number, 2 * PATCH_LAT_EXTENT + 1, 0), azimuth_reaches[present_parallel_number], head_logit_scales)
    mixture = lax.map(attend_global, row_ids)
    output = jnp.dot(mixture.reshape(-1, CHANNELS), final_projector, preferred_element_type=jnp.float32)
    return (hidden + output.reshape(hidden.shape)).astype(jnp.bfloat16)
```

```python
import functools

import jax
import jax.numpy as jnp
from jax import lax
from jax.experimental import pallas as pl
from jax.experimental.pallas import tpu as pltpu
from jax.sharding import PartitionSpec as P

HEAD_COUNT = 8
HEAD_WIDTH = 32
BASIS_COUNT = 9
CONV_REACH = 4
PATCH_LAT_EXTENT = 2
DISC_REACH = 8
TAPS = 2 * CONV_REACH + 1
DISC_ROWS = 2 * PATCH_LAT_EXTENT + 1
EPSILON = 1e-06
HALO = PATCH_LAT_EXTENT + 1
BAND = 64
WINDOW = BAND + 16
QUERIES = 16
KEYS = QUERIES + 2 * DISC_REACH
FILTER_ROWS = 16
F32 = jnp.float32
BF16 = jnp.bfloat16


def scaled_norm(values, gain):
    inverse = lax.rsqrt(jnp.mean(values * values, axis=-1, keepdims=True) + EPSILON)
    return values * inverse * gain


def head_unit(values, ones):
    squares = values * values
    high = squares.astype(BF16)
    low = (squares - high.astype(F32)).astype(BF16)
    total = jnp.dot(high, ones, preferred_element_type=F32) + jnp.dot(
        low, ones, preferred_element_type=F32
    )
    return values * lax.rsqrt(total + EPSILON)


def wrapped(values, before, after):
    parts = [values[values.shape[0] - before :], values, values[:after]]
    return jnp.concatenate(parts, axis=0)


def window_kernel(
    rows,
    longitudes,
    flags,
    reaches,
    scales,
    local,
    low,
    high,
    flipped,
    conv_gain,
    mixer,
    attn_gain,
    projector,
    final,
    out,
    raw,
    normed,
    filters,
    bands,
    basis,
    hidden,
    attn_in,
    keys,
    values,
    queries,
    bias,
    mixture,
):
    channels = local.shape[1]
    half = longitudes // 2
    first = flags[0] > 0
    last = flags[1] > 0
    halo_base = HALO * longitudes

    def local_row(row):
        return local[row * longitudes : (row + 1) * longitudes, :]

    def rolled(row):
        block = local_row(row)
        return jnp.concatenate([block[half:], block[:half]], axis=0)

    for step in range(HALO):
        there = low[step * longitudes : (step + 1) * longitudes, :]
        raw[step] = jnp.where(first, rolled(HALO - 1 - step), there)
        there = high[step * longitudes : (step + 1) * longitudes, :]
        raw[HALO + rows + step] = jnp.where(last, rolled(rows - 1 - step), there)
    for row in range(rows):
        raw[HALO + row] = local_row(row)

    def norm_row(row, carry):
        block = scaled_norm(raw[row].astype(F32), conv_gain[...])
        normed[row] = wrapped(block, 8, 24).astype(BF16)
        return carry

    lax.fori_loop(0, rows + 2 * HALO, norm_row, 0)

    def filter_rows(ref, base, row):
        start = base + row * FILTER_ROWS
        return ref[start : start + FILTER_ROWS, :].astype(F32)

    for step in range(2):
        mine = filter_rows(flipped, 0, 1 - step)
        there = filter_rows(low, halo_base, 1 + step)
        filters[step] = jnp.where(first, mine, there)
        mine = filter_rows(flipped, 0, rows - 1 - step)
        there = filter_rows(high, halo_base, step)
        filters[2 + rows + step] = jnp.where(last, mine, there)
    for row in range(rows):
        filters[2 + row] = filter_rows(local, rows * longitudes, row)

    def conv_row(row, carry):
        for k in range(BASIS_COUNT):
            line = jnp.broadcast_to(filters[row, k : k + 1, :], (BAND, channels))
            line = pltpu.roll(line, 0, 1, stride=1, stride_axis=0)
            bands[k * BAND : (k + 1) * BAND, :] = line.astype(BF16)
        for block in range(longitudes // BAND):
            start = block * BAND
            window = jnp.concatenate(
                [
                    normed[row, start : start + WINDOW, :],
                    normed[row + 1, start : start + WINDOW, :],
                    normed[row + 2, start : start + WINDOW + 16, :],
                ],
                axis=0,
            )
            sums = jnp.dot(bands[...], window, preferred_element_type=F32).astype(BF16)
            for k in range(BASIS_COUNT):
                basis[start : start + BAND, k * channels : (k + 1) * channels] = sums[
                    k * BAND : (k + 1) * BAND
                ]
        total = raw[row + 1].astype(F32) + jnp.dot(
            basis[...], mixer[...], preferred_element_type=F32
        )
        hidden[row] = total
        attn_in[row] = scaled_norm(total, attn_gain[...]).astype(BF16)
        return carry

    lax.fori_loop(0, rows + 2 * PATCH_LAT_EXTENT, conv_row, 0)

    head_of_lane = lax.broadcasted_iota(jnp.int32, (channels, channels), 1) // HEAD_WIDTH
    head_of_row = lax.broadcasted_iota(jnp.int32, (channels, channels), 0) // HEAD_WIDTH
    ones = jnp.where(head_of_lane == head_of_row, 1.0, 0.0).astype(BF16)

    def key_row(row, carry):
        both = jnp.dot(
            attn_in[row], projector[:, channels : 3 * channels], preferred_element_type=F32
        )
        rounded = both.astype(BF16).astype(F32)
        unit = head_unit(rounded[:, :channels], ones)
        keys[row] = wrapped(unit, DISC_REACH, DISC_REACH).astype(BF16)
        values[row] = wrapped(rounded[:, channels:], DISC_REACH, DISC_REACH).astype(BF16)
        return carry

    lax.fori_loop(0, rows + 2 * PATCH_LAT_EXTENT, key_row, 0)

    lanes = HEAD_COUNT * QUERIES
    disc = DISC_ROWS * KEYS

    def query_row(row, carry):
        probe = jnp.dot(
            attn_in[row + PATCH_LAT_EXTENT],
            projector[:, :channels],
            preferred_element_type=F32,
        )
        queries[row] = head_unit(probe.astype(BF16).astype(F32), ones).astype(BF16)
        key_at = lax.broadcasted_iota(jnp.int32, (KEYS, lanes), 0)
        query_at = lax.broadcasted_iota(jnp.int32, (KEYS, lanes), 1) % QUERIES
        distance = jnp.abs(key_at - DISC_REACH - query_at)
        for a in range(DISC_ROWS):
            bias[row, a * KEYS : (a + 1) * KEYS, :] = jnp.where(
                distance <= reaches[row, a], 0.0, -1e30
            ).astype(F32)
        return carry

    lax.fori_loop(0, rows, query_row, 0)

    lane_head = lax.broadcasted_iota(jnp.int32, (1, lanes), 1) // QUERIES
    scale = jnp.zeros((1, lanes), F32)
    for h in range(HEAD_COUNT):
        scale = jnp.where(lane_head == h, scales[h], scale)
    channel_head = lax.broadcasted_iota(jnp.int32, (QUERIES, channels), 1) // HEAD_WIDTH

    unroll = 4
    per_row = longitudes // (QUERIES * unroll)

    def attend(step, carry):
        row = step // per_row
        base = (step % per_row) * (QUERIES * unroll)
        for u in range(unroll):
            start = pl.multiple_of(base + u * QUERIES, QUERIES)
            probe = queries[row, pl.ds(start, QUERIES), :]
            spread = jnp.concatenate(
                [jnp.where(channel_head == h, probe, jnp.zeros_like(probe)) for h in range(HEAD_COUNT)],
                axis=0,
            )
            near_keys = jnp.concatenate(
                [keys[row + a, pl.ds(start, KEYS), :] for a in range(DISC_ROWS)], axis=0
            )
            near_values = jnp.concatenate(
                [values[row + a, pl.ds(start, KEYS), :] for a in range(DISC_ROWS)], axis=0
            )
            scores = lax.dot_general(
                near_keys, spread, (((1,), (1,)), ((), ())), preferred_element_type=F32
            )
            scores = scores + bias[row]
            peak = jnp.max(scores, axis=0, keepdims=True)
            weights = jnp.exp((scores - peak) * scale)
            total = jnp.sum(weights, axis=0, keepdims=True)
            weights = (weights * (1.0 / total)).astype(BF16)
            mixed = lax.dot_general(
                weights, near_values, (((0,), (0,)), ((), ())), preferred_element_type=F32
            )
            result = jnp.zeros((QUERIES, channels), F32)
            for h in range(HEAD_COUNT):
                result = jnp.where(
                    channel_head == h, mixed[h * QUERIES : (h + 1) * QUERIES], result
                )
            mixture[row, pl.ds(start, QUERIES), :] = result.astype(BF16)
        return carry

    lax.fori_loop(0, rows * per_row, attend, 0)

    def finish(row, carry):
        product = jnp.dot(mixture[row], final[...], preferred_element_type=F32)
        out[row] = (hidden[row + PATCH_LAT_EXTENT] + product).astype(BF16)
        return carry

    lax.fori_loop(0, rows, finish, 0)


def filter_lines(profiles, reaches, flip):
    count = profiles.shape[0]
    offsets = jnp.abs(jnp.arange(TAPS, dtype=jnp.int32) - CONV_REACH)
    limits = reaches[:, PATCH_LAT_EXTENT - 1 : PATCH_LAT_EXTENT + 2]
    visible = offsets[None, None, :] <= limits[:, :, None]
    shaped = profiles.reshape(count, BASIS_COUNT, 3, TAPS)
    masked = jnp.where(visible[:, None], shaped, 0.0).astype(BF16)
    if flip:
        masked = masked[:, :, ::-1, :]
    edge = WINDOW - BAND - TAPS - CONV_REACH
    lines = jnp.pad(masked, ((0, 0), (0, 0), (0, 0), (CONV_REACH, BAND + edge)))
    lines = lines.reshape(count, BASIS_COUNT, 3 * WINDOW)
    lines = jnp.pad(lines, ((0, 0), (0, FILTER_ROWS - BASIS_COUNT), (0, 256 - 3 * WINDOW)))
    return lines.reshape(count * FILTER_ROWS, 256)


def on_device(
    grid_inputs,
    stencil_prenorm_scale,
    patch_kernel_profiles,
    channel_mixer_tensor,
    softmax_prenorm_scale,
    probe_lookup_content_projector,
    head_logit_scales,
    final_projector,
    azimuth_reaches,
):
    rows, longitudes, channels = grid_inputs.shape
    assert rows >= HALO and longitudes % BAND == 0 and channels == 256
    flat = grid_inputs.reshape(rows * longitudes, channels)
    lines = filter_lines(patch_kernel_profiles, azimuth_reaches, False)
    flipped = filter_lines(patch_kernel_profiles, azimuth_reaches, True)
    local = jnp.concatenate([flat, lines], axis=0)
    if rows == HALO:
        upward = downward = local
    else:
        upward = jnp.concatenate([flat[-HALO * longitudes :], lines[-HALO * FILTER_ROWS :]], axis=0)
        downward = jnp.concatenate([flat[: HALO * longitudes], lines[: HALO * FILTER_ROWS]], axis=0)
    count = lax.axis_size("band")
    position = lax.axis_index("band")
    forward = [(i, i + 1) for i in range(count - 1)]
    backward = [(target, source) for source, target in forward]
    low = lax.ppermute(upward, "band", forward)
    high = lax.ppermute(downward, "band", backward)
    flags = jnp.stack([position == 0, position == count - 1]).astype(jnp.int32)
    wide = rows + 2 * PATCH_LAT_EXTENT
    smem = pl.BlockSpec(memory_space=pltpu.SMEM)
    vmem = pl.BlockSpec(memory_space=pltpu.VMEM)
    return pl.pallas_call(
        functools.partial(window_kernel, rows, longitudes),
        out_shape=jax.ShapeDtypeStruct(grid_inputs.shape, BF16),
        in_specs=[smem] * 3 + [vmem] * 9,
        out_specs=vmem,
        scratch_shapes=[
            pltpu.VMEM((rows + 2 * HALO, longitudes, channels), BF16),
            pltpu.VMEM((rows + 2 * HALO, longitudes + 32, channels), BF16),
            pltpu.VMEM((wide, FILTER_ROWS, channels), F32),
            pltpu.VMEM((BASIS_COUNT * BAND, channels), BF16),
            pltpu.VMEM((longitudes, BASIS_COUNT * channels), BF16),
            pltpu.VMEM((wide, longitudes, channels), F32),
            pltpu.VMEM((wide, longitudes, channels), BF16),
            pltpu.VMEM((wide, longitudes + 2 * DISC_REACH, channels), BF16),
            pltpu.VMEM((wide, longitudes + 2 * DISC_REACH, channels), BF16),
            pltpu.VMEM((rows, longitudes, channels), BF16),
            pltpu.VMEM((rows, DISC_ROWS * KEYS, HEAD_COUNT * QUERIES), F32),
            pltpu.VMEM((rows, longitudes, channels), BF16),
        ],
        compiler_params=pltpu.CompilerParams(vmem_limit_bytes=56 * 1024 * 1024),
    )(
        flags,
        azimuth_reaches,
        head_logit_scales,
        local,
        low,
        high,
        flipped,
        stencil_prenorm_scale.reshape(1, channels),
        channel_mixer_tensor,
        softmax_prenorm_scale.reshape(1, channels),
        probe_lookup_content_projector,
        final_projector,
    )


def solution(mesh):
    placed = (
        P(("members", "band"), None, None),
        P(),
        P("band", None, None),
        P(),
        P(),
        P(),
        P(),
        P(),
        P("band", None),
    )
    return jax.shard_map(
        on_device,
        mesh=mesh,
        in_specs=placed,
        out_specs=P(("members", "band"), None, None),
        check_vma=False,
    )
```

```python
import functools

import jax
import jax.numpy as jnp
from jax import lax
from jax.experimental import pallas as pl
from jax.experimental.pallas import tpu as pltpu
from jax.sharding import PartitionSpec as P

HEAD_COUNT = 8
HEAD_WIDTH = 32
BASIS_COUNT = 9
CONV_REACH = 4
PATCH_LAT_EXTENT = 2
DISC_REACH = 8
TAPS = 2 * CONV_REACH + 1
DISC_ROWS = 2 * PATCH_LAT_EXTENT + 1
EPSILON = 1e-06
HALO = PATCH_LAT_EXTENT + 1
BAND = 64
WINDOW = BAND + 16
QUERIES = 16
KEYS = QUERIES + 2 * DISC_REACH
FILTER_ROWS = 16
F32 = jnp.float32
BF16 = jnp.bfloat16


def scaled_norm(values, gain):
    inverse = lax.rsqrt(jnp.mean(values * values, axis=-1, keepdims=True) + EPSILON)
    return values * inverse * gain


def head_unit(values, ones):
    squares = values * values
    high = squares.astype(BF16)
    low = (squares - high.astype(F32)).astype(BF16)
    total = jnp.dot(high, ones, preferred_element_type=F32) + jnp.dot(
        low, ones, preferred_element_type=F32
    )
    return values * lax.rsqrt(total + EPSILON)


def wrapped(values, before, after):
    parts = [values[values.shape[0] - before :], values, values[:after]]
    return jnp.concatenate(parts, axis=0)


def band_rows(filters, row, bands):
    channels = filters.shape[-1]
    for k in range(BASIS_COUNT):
        line = jnp.broadcast_to(filters[row, k : k + 1, :], (BAND, channels))
        line = pltpu.roll(line, 0, 1, stride=1, stride_axis=0)
        bands[k * BAND : (k + 1) * BAND, :] = line.astype(BF16)


def conv_row(row, raw, normed, filters, mixer, bands, basis, shift):
    longitudes, channels = raw.shape[1:]
    band_rows(filters, row + shift, bands)
    for block in range(longitudes // BAND):
        start = block * BAND
        window = jnp.concatenate(
            [
                normed[row, start : start + WINDOW, :],
                normed[row + 1, start : start + WINDOW, :],
                normed[row + 2, start : start + WINDOW + 16, :],
            ],
            axis=0,
        )
        sums = jnp.dot(bands[...], window, preferred_element_type=F32).astype(BF16)
        for k in range(BASIS_COUNT):
            basis[start : start + BAND, k * channels : (k + 1) * channels] = sums[
                k * BAND : (k + 1) * BAND
            ]
    return raw[row + 1].astype(F32) + jnp.dot(
        basis[...], mixer[...], preferred_element_type=F32
    )


def norm_rows(count, raw, normed, gain):
    def norm_row(row, carry):
        block = scaled_norm(raw[row].astype(F32), gain[...])
        normed[row] = wrapped(block, 8, 24).astype(BF16)
        return carry

    lax.fori_loop(0, count, norm_row, 0)


def head_ones(channels):
    head_of_lane = lax.broadcasted_iota(jnp.int32, (channels, channels), 1) // HEAD_WIDTH
    head_of_row = lax.broadcasted_iota(jnp.int32, (channels, channels), 0) // HEAD_WIDTH
    return jnp.where(head_of_lane == head_of_row, 1.0, 0.0).astype(BF16)


def key_row(block, projector, ones):
    channels = block.shape[1]
    both = jnp.dot(block, projector[:, channels : 3 * channels], preferred_element_type=F32)
    rounded = both.astype(BF16).astype(F32)
    unit = head_unit(rounded[:, :channels], ones)
    return (
        wrapped(unit, DISC_REACH, DISC_REACH).astype(BF16),
        wrapped(rounded[:, channels:], DISC_REACH, DISC_REACH).astype(BF16),
    )


def query_row(block, projector, ones):
    channels = block.shape[1]
    probe = jnp.dot(block, projector[:, :channels], preferred_element_type=F32)
    return head_unit(probe.astype(BF16).astype(F32), ones).astype(BF16)


def lines_kernel(rows, reaches, profiles, source, payload, flipped, pad):
    size = source.shape[0]
    payload[:size, :] = source[...]
    shape = (FILTER_ROWS, pad.shape[1])
    lane = lax.broadcasted_iota(jnp.int32, shape, 1)
    for row in range(rows):
        pad[...] = jnp.zeros(shape, F32)
        pad[:BASIS_COUNT, : 3 * TAPS] = profiles[row]
        block = pad[...]
        straight = jnp.zeros(shape, F32)
        mirrored = jnp.zeros(shape, F32)
        for a in range(3):
            distance = jnp.abs(lane - (a * TAPS + CONV_REACH))
            seen = distance <= jnp.minimum(reaches[row, PATCH_LAT_EXTENT - 1 + a], CONV_REACH)
            part = jnp.where(seen, block, 0.0)
            shift = a * WINDOW + CONV_REACH - a * TAPS
            straight = straight + pltpu.roll(part, shift, 1)
            shift = (2 - a) * WINDOW + CONV_REACH - a * TAPS
            mirrored = mirrored + pltpu.roll(part, shift % pad.shape[1], 1)
        base = row * FILTER_ROWS
        payload[size + base : size + base + FILTER_ROWS, :] = straight.astype(BF16)
        flipped[base : base + FILTER_ROWS, :] = mirrored.astype(BF16)


def near_kernel(
    rows,
    longitudes,
    flags,
    local,
    partner,
    conv_gain,
    mixer,
    attn_gain,
    projector,
    hidden,
    keys,
    values,
    queries,
    raw,
    normed,
    filters,
    bands,
    basis,
):
    channels = local.shape[1]
    even = flags[2]
    mine = (1 - even) * HALO
    other = HALO - mine
    for row in range(HALO):
        at = row * longitudes
        raw[mine + row] = local[at : at + longitudes, :]
        raw[other + row] = partner[at : at + longitudes, :]
        at = HALO * longitudes + row * FILTER_ROWS
        filters[mine + row] = local[at : at + FILTER_ROWS, :].astype(F32)
        filters[other + row] = partner[at : at + FILTER_ROWS, :].astype(F32)
    norm_rows(2 * HALO, raw, normed, conv_gain)
    ones = head_ones(channels)

    def conv_step(row, carry):
        total = conv_row(row, raw, normed, filters, mixer, bands, basis, 1)
        hidden[row] = total
        block = scaled_norm(total, attn_gain[...]).astype(BF16)
        keys[row], values[row] = key_row(block, projector, ones)
        queries[row] = query_row(block, projector, ones)
        return carry

    lax.fori_loop(0, 2 * HALO - 2, conv_step, 0)


def far_kernel(
    rows,
    longitudes,
    flags,
    reaches,
    scales,
    local,
    cross,
    cross_lines,
    flipped,
    conv_gain,
    mixer,
    attn_gain,
    projector,
    final,
    near_hidden,
    near_keys,
    near_values,
    near_queries,
    out,
    raw,
    normed,
    filters,
    bands,
    basis,
    hidden,
    keys,
    values,
    queries,
    bias,
    mixture,
):
    channels = local.shape[1]
    half = longitudes // 2
    pole = flags[0] + flags[1] > 0
    even = flags[2]
    wide = rows + 2 * PATCH_LAT_EXTENT
    near = 2 * HALO - 2
    far = wide - near

    def local_row(row):
        return local[row * longitudes : (row + 1) * longitudes, :]

    def rolled(row):
        block = local_row(row)
        return jnp.concatenate([block[half:], block[:half]], axis=0)

    far_base = (1 - even) * 2
    for step in range(HALO):
        there = cross[step * longitudes : (step + 1) * longitudes, :]
        raw[far_base + step] = jnp.where(pole, rolled(HALO - 1 - step), there)
    own_base = even * HALO
    for step in range(2):
        lower, upper = local_row(step), local_row(step + 1)
        raw[own_base + step] = jnp.where(even > 0, lower, upper)

    def lines(ref, row):
        return ref[row * FILTER_ROWS : (row + 1) * FILTER_ROWS, :].astype(F32)

    base = rows * longitudes // FILTER_ROWS
    for u in range(far):
        from_even = lines(local, base) if u == far - 1 else jnp.where(
            pole, lines(flipped, far - 2 - u), lines(cross_lines, u + 1)
        )
        from_odd = lines(local, base + rows - 1) if u == 0 else jnp.where(
            pole, lines(flipped, rows - u), lines(cross_lines, u - 1)
        )
        filters[u] = jnp.where(even > 0, from_even, from_odd)
    norm_rows(far + 2, raw, normed, conv_gain)
    ones = head_ones(channels)
    far_slot = (1 - even) * near
    near_slot = even * far

    def copy_near(row, carry):
        hidden[near_slot + row] = near_hidden[row]
        keys[near_slot + row] = near_keys[row]
        values[near_slot + row] = near_values[row]
        queries[near_slot + row] = near_queries[row]
        return carry

    lax.fori_loop(0, near, copy_near, 0)

    def conv_step(row, carry):
        total = conv_row(row, raw, normed, filters, mixer, bands, basis, 0)
        slot = far_slot + row
        hidden[slot] = total
        block = scaled_norm(total, attn_gain[...]).astype(BF16)
        keys[slot], values[slot] = key_row(block, projector, ones)
        queries[slot] = query_row(block, projector, ones)
        return carry

    lax.fori_loop(0, far, conv_step, 0)

    lanes = HEAD_COUNT * QUERIES

    def bias_row(row, carry):
        key_at = lax.broadcasted_iota(jnp.int32, (KEYS, lanes), 0)
        query_at = lax.broadcasted_iota(jnp.int32, (KEYS, lanes), 1) % QUERIES
        distance = jnp.abs(key_at - DISC_REACH - query_at)
        for a in range(DISC_ROWS):
            bias[row, a * KEYS : (a + 1) * KEYS, :] = jnp.where(
                distance <= reaches[row, a], 0.0, -1e30
            ).astype(F32)
        return carry

    lax.fori_loop(0, rows, bias_row, 0)

    lane_head = lax.broadcasted_iota(jnp.int32, (1, lanes), 1) // QUERIES
    scale = jnp.zeros((1, lanes), F32)
    for h in range(HEAD_COUNT):
        scale = jnp.where(lane_head == h, scales[h], scale)
    channel_head = lax.broadcasted_iota(jnp.int32, (QUERIES, channels), 1) // HEAD_WIDTH

    unroll = 4
    per_row = longitudes // (QUERIES * unroll)

    def attend(step, carry):
        row = step // per_row
        base = (step % per_row) * (QUERIES * unroll)
        for u in range(unroll):
            start = pl.multiple_of(base + u * QUERIES, QUERIES)
            probe = queries[row + PATCH_LAT_EXTENT, pl.ds(start, QUERIES), :]
            spread = jnp.concatenate(
                [jnp.where(channel_head == h, probe, jnp.zeros_like(probe)) for h in range(HEAD_COUNT)],
                axis=0,
            )
            near_k = jnp.concatenate(
                [keys[row + a, pl.ds(start, KEYS), :] for a in range(DISC_ROWS)], axis=0
            )
            near_v = jnp.concatenate(
                [values[row + a, pl.ds(start, KEYS), :] for a in range(DISC_ROWS)], axis=0
            )
            scores = lax.dot_general(
                near_k, spread, (((1,), (1,)), ((), ())), preferred_element_type=F32
            )
            scores = scores + bias[row]
            peak = jnp.max(scores, axis=0, keepdims=True)
            weights = jnp.exp((scores - peak) * scale)
            total = jnp.sum(weights, axis=0, keepdims=True)
            weights = (weights * (1.0 / total)).astype(BF16)
            mixed = lax.dot_general(
                weights, near_v, (((0,), (0,)), ((), ())), preferred_element_type=F32
            )
            result = jnp.zeros((QUERIES, channels), F32)
            for h in range(HEAD_COUNT):
                result = jnp.where(
                    channel_head == h, mixed[h * QUERIES : (h + 1) * QUERIES], result
                )
            mixture[row, pl.ds(start, QUERIES), :] = result.astype(BF16)
        return carry

    lax.fori_loop(0, rows * per_row, attend, 0)

    def finish(row, carry):
        product = jnp.dot(mixture[row], final[...], preferred_element_type=F32)
        out[row] = (hidden[row + PATCH_LAT_EXTENT] + product).astype(BF16)
        return carry

    lax.fori_loop(0, rows, finish, 0)


def on_device(
    grid_inputs,
    stencil_prenorm_scale,
    patch_kernel_profiles,
    channel_mixer_tensor,
    softmax_prenorm_scale,
    probe_lookup_content_projector,
    head_logit_scales,
    final_projector,
    azimuth_reaches,
):
    rows, longitudes, channels = grid_inputs.shape
    count = lax.axis_size("band")
    assert rows == HALO and longitudes % BAND == 0 and channels == 256 and count % 2 == 0
    position = lax.axis_index("band")
    within = [(i, i ^ 1) for i in range(count)]
    across = [pair for i in range(1, count - 1, 2) for pair in ((i, i + 1), (i + 1, i))]
    flat = grid_inputs.reshape(rows * longitudes, channels)
    cross = lax.ppermute(flat, "band", across)
    smem = pl.BlockSpec(memory_space=pltpu.SMEM)
    vmem = pl.BlockSpec(memory_space=pltpu.VMEM)
    limit = pltpu.CompilerParams(vmem_limit_bytes=48 * 1024 * 1024)
    size = rows * longitudes
    local, flipped = pl.pallas_call(
        functools.partial(lines_kernel, rows),
        out_shape=(
            jax.ShapeDtypeStruct((size + rows * FILTER_ROWS, channels), BF16),
            jax.ShapeDtypeStruct((rows * FILTER_ROWS, channels), BF16),
        ),
        in_specs=[smem, vmem, vmem],
        out_specs=(vmem, vmem),
        scratch_shapes=[pltpu.VMEM((FILTER_ROWS, channels), F32)],
    )(azimuth_reaches, patch_kernel_profiles, flat)
    partner = lax.ppermute(local, "band", within)
    cross_lines = lax.ppermute(local[size:], "band", across)
    flags = jnp.stack([position == 0, position == count - 1, position % 2 == 0]).astype(jnp.int32)
    conv_gain = stencil_prenorm_scale.reshape(1, channels)
    attn_gain = softmax_prenorm_scale.reshape(1, channels)
    near = 2 * HALO - 2
    wide = rows + 2 * PATCH_LAT_EXTENT
    padded = longitudes + 2 * DISC_REACH
    shared = [
        pltpu.VMEM((BASIS_COUNT * BAND, channels), BF16),
        pltpu.VMEM((longitudes, BASIS_COUNT * channels), BF16),
    ]
    near_state = pl.pallas_call(
        functools.partial(near_kernel, rows, longitudes),
        out_shape=(
            jax.ShapeDtypeStruct((near, longitudes, channels), F32),
            jax.ShapeDtypeStruct((near, padded, channels), BF16),
            jax.ShapeDtypeStruct((near, padded, channels), BF16),
            jax.ShapeDtypeStruct((near, longitudes, channels), BF16),
        ),
        in_specs=[smem] + [vmem] * 6,
        out_specs=(vmem,) * 4,
        scratch_shapes=[
            pltpu.VMEM((2 * HALO, longitudes, channels), BF16),
            pltpu.VMEM((2 * HALO, longitudes + 32, channels), BF16),
            pltpu.VMEM((2 * HALO, FILTER_ROWS, channels), F32),
        ]
        + shared,
        compiler_params=limit,
        cost_estimate=pl.CostEstimate(flops=8 * 10**9, bytes_accessed=8 * 10**6, transcendentals=0),
    )(flags, local, partner, conv_gain, channel_mixer_tensor, attn_gain, probe_lookup_content_projector)
    return pl.pallas_call(
        functools.partial(far_kernel, rows, longitudes),
        out_shape=jax.ShapeDtypeStruct(grid_inputs.shape, BF16),
        in_specs=[smem] * 3 + [vmem] * 13,
        out_specs=vmem,
        scratch_shapes=[
            pltpu.VMEM((HALO + 2, longitudes, channels), BF16),
            pltpu.VMEM((HALO + 2, longitudes + 32, channels), BF16),
            pltpu.VMEM((HALO, FILTER_ROWS, channels), F32),
        ]
        + shared
        + [
            pltpu.VMEM((wide, longitudes, channels), F32),
            pltpu.VMEM((wide, padded, channels), BF16),
            pltpu.VMEM((wide, padded, channels), BF16),
            pltpu.VMEM((wide, longitudes, channels), BF16),
            pltpu.VMEM((rows, DISC_ROWS * KEYS, HEAD_COUNT * QUERIES), F32),
            pltpu.VMEM((rows, longitudes, channels), BF16),
        ],
        compiler_params=limit,
        cost_estimate=pl.CostEstimate(flops=10**10, bytes_accessed=8 * 10**6, transcendentals=10**6),
    )(
        flags,
        azimuth_reaches,
        head_logit_scales,
        local,
        cross,
        cross_lines,
        flipped,
        conv_gain,
        channel_mixer_tensor,
        attn_gain,
        probe_lookup_content_projector,
        final_projector,
        *near_state,
    )


def solution(mesh):
    placed = (
        P(("members", "band"), None, None),
        P(),
        P("band", None, None),
        P(),
        P(),
        P(),
        P(),
        P(),
        P("band", None),
    )
    return jax.shard_map(
        on_device,
        mesh=mesh,
        in_specs=placed,
        out_specs=P(("members", "band"), None, None),
        check_vma=False,
    )
```

```python
import functools

import jax
import jax.numpy as jnp
from jax import lax
from jax.experimental import pallas as pl
from jax.experimental.pallas import tpu as pltpu
from jax.sharding import PartitionSpec as P

HEAD_COUNT = 8
HEAD_WIDTH = 32
BASIS_COUNT = 9
CONV_REACH = 4
PATCH_LAT_EXTENT = 2
DISC_REACH = 8
TAPS = 2 * CONV_REACH + 1
DISC_ROWS = 2 * PATCH_LAT_EXTENT + 1
EPSILON = 1e-06
HALO = PATCH_LAT_EXTENT + 1
BAND = 64
WINDOW = BAND + 16
QUERIES = 16
KEYS = QUERIES + 2 * DISC_REACH
FILTER_ROWS = 16
UNROLL = 12
VMEM_LIMIT = 67043328
F32 = jnp.float32
BF16 = jnp.bfloat16


def scaled_norm(values, gain):
    inverse = lax.rsqrt(jnp.mean(values * values, axis=-1, keepdims=True) + EPSILON)
    return values * inverse * gain


def head_unit(values, ones):
    squares = values * values
    high = squares.astype(BF16)
    low = (squares - high.astype(F32)).astype(BF16)
    total = jnp.dot(high, ones, preferred_element_type=F32) + jnp.dot(
        low, ones, preferred_element_type=F32
    )
    return values * lax.rsqrt(total + EPSILON)


def wrapped(values, before, after):
    parts = [values[values.shape[0] - before :], values, values[:after]]
    return jnp.concatenate(parts, axis=0)


def band_rows(filters, row, bands):
    channels = filters.shape[-1]
    for k in range(BASIS_COUNT):
        line = jnp.broadcast_to(filters[row, k : k + 1, :], (BAND, channels))
        line = pltpu.roll(line, 0, 1, stride=1, stride_axis=0)
        bands[k * BAND : (k + 1) * BAND, :] = line.astype(BF16)


def band_row(row, line_row, normed, filters, bands, basis):
    longitudes, channels = basis.shape[0], filters.shape[-1]
    band_rows(filters, line_row, bands)
    for block in range(longitudes // BAND):
        start = block * BAND
        window = jnp.concatenate(
            [
                normed[row, start : start + WINDOW, :],
                normed[row + 1, start : start + WINDOW, :],
                normed[row + 2, start : start + WINDOW + 16, :],
            ],
            axis=0,
        )
        sums = jnp.dot(bands[...], window, preferred_element_type=F32).astype(BF16)
        for k in range(BASIS_COUNT):
            basis[start : start + BAND, k * channels : (k + 1) * channels] = sums[
                k * BAND : (k + 1) * BAND
            ]


def mix_row(block, basis, mixer):
    return block.astype(F32) + jnp.dot(basis[...], mixer[...], preferred_element_type=F32)


def norm_rows(count, raw, normed, gain):
    def norm_row(row, carry):
        block = scaled_norm(raw[row].astype(F32), gain[...])
        normed[row] = wrapped(block, 8, 24).astype(BF16)
        return carry

    lax.fori_loop(0, count, norm_row, 0)


def head_ones(channels):
    head_of_lane = lax.broadcasted_iota(jnp.int32, (channels, channels), 1) // HEAD_WIDTH
    head_of_row = lax.broadcasted_iota(jnp.int32, (channels, channels), 0) // HEAD_WIDTH
    return jnp.where(head_of_lane == head_of_row, 1.0, 0.0).astype(BF16)


def key_row(block, projector, ones):
    channels = block.shape[1]
    both = jnp.dot(block, projector[:, channels : 3 * channels], preferred_element_type=F32)
    rounded = both.astype(BF16).astype(F32)
    unit = head_unit(rounded[:, :channels], ones)
    return (
        wrapped(unit, DISC_REACH, DISC_REACH).astype(BF16),
        wrapped(rounded[:, channels:], DISC_REACH, DISC_REACH).astype(BF16),
    )


def query_row(block, projector, ones):
    channels = block.shape[1]
    probe = jnp.dot(block, projector[:, :channels], preferred_element_type=F32)
    return head_unit(probe.astype(BF16).astype(F32), ones).astype(BF16)


def lines_kernel(rows, reaches, profiles, source, payload, lines, staged, pad, sems):
    size = source.shape[0]
    fetch = pltpu.make_async_copy(source, staged.at[pl.ds(0, size), :], sems.at[0])
    fetch.start()
    shape = (FILTER_ROWS, pad.shape[1])
    lane = lax.broadcasted_iota(jnp.int32, shape, 1)
    for row in range(rows):
        pad[...] = jnp.zeros(shape, F32)
        pad[:BASIS_COUNT, : 3 * TAPS] = profiles[:, row, :]
        block = pad[...]
        straight = jnp.zeros(shape, F32)
        mirrored = jnp.zeros(shape, F32)
        for a in range(3):
            distance = jnp.abs(lane - (a * TAPS + CONV_REACH))
            seen = distance <= jnp.minimum(reaches[row, PATCH_LAT_EXTENT - 1 + a], CONV_REACH)
            part = jnp.where(seen, block, 0.0)
            shift = a * WINDOW + CONV_REACH - a * TAPS
            straight = straight + pltpu.roll(part, shift, 1)
            shift = (2 - a) * WINDOW + CONV_REACH - a * TAPS
            mirrored = mirrored + pltpu.roll(part, shift % pad.shape[1], 1)
        base = row * FILTER_ROWS
        straight = straight.astype(BF16)
        staged[size + base : size + base + FILTER_ROWS, :] = straight
        lines[0, base : base + FILTER_ROWS, :] = straight
        lines[1, base : base + FILTER_ROWS, :] = mirrored.astype(BF16)
    fetch.wait()
    send = pltpu.make_async_copy(staged, payload, sems.at[1])
    send.start()
    send.wait()


def fetches(pairs, sems):
    copies = [pltpu.make_async_copy(a, b, sems.at[i]) for i, (a, b) in enumerate(pairs)]
    for copy in copies:
        copy.start()
    return copies


def near_kernel(
    rows,
    longitudes,
    local,
    lines_hbm,
    partner,
    conv_gain_hbm,
    mixer_hbm,
    attn_gain_hbm,
    projector_hbm,
    hidden_out,
    keys_out,
    values_out,
    queries_out,
    lines,
    there,
    conv_gain,
    mixer,
    attn_gain,
    projector,
    raw,
    normed,
    filters,
    bands,
    basis,
    hidden,
    attn_in,
    keys,
    values,
    queries,
    sems,
    done,
):
    channels = raw.shape[2]
    size = rows * longitudes
    even = 1 - lax.rem(lax.axis_index("band"), 2)
    mine = (1 - even) * HALO
    other = HALO - mine
    near = 2 * HALO - 2
    own = (1 - even) * 2
    copies = fetches(
        [(local, raw.at[pl.ds(mine, HALO)])]
        + [
            (partner.at[pl.ds(row * longitudes, longitudes)], raw.at[other + row])
            for row in range(HALO)
        ]
        + [
            (conv_gain_hbm, conv_gain),
            (lines_hbm, lines),
            (partner.at[pl.ds(size, HALO * FILTER_ROWS)], there),
            (mixer_hbm, mixer),
            (attn_gain_hbm, attn_gain),
            (projector_hbm, projector),
        ],
        sems,
    )
    for copy in copies[:7]:
        copy.wait()
    for row in range(HALO):
        at = row * FILTER_ROWS
        filters[mine + row] = lines[0, at : at + FILTER_ROWS, :].astype(F32)
        filters[other + row] = there[at : at + FILTER_ROWS, :].astype(F32)
    norm_rows(2 * HALO, raw, normed, conv_gain)
    ones = head_ones(channels)
    for row in range(near):
        band_row(row, row + 1, normed, filters, bands.at[row % 2], basis.at[row])
    for copy in copies[7:]:
        copy.wait()
    for row in range(near):
        total = mix_row(raw[row + 1], basis.at[row], mixer)
        hidden[row] = total
        attn_in[row] = scaled_norm(total, attn_gain[...]).astype(BF16)
    sends = [pltpu.make_async_copy(hidden.at[pl.ds(own, 2)], hidden_out, done.at[0])]
    sends[0].start()
    for row in range(near):
        keys[row], values[row] = key_row(attn_in[row], projector, ones)
        sends += fetches(
            [(keys.at[row], keys_out.at[row]), (values.at[row], values_out.at[row])],
            done.at[pl.ds(1 + 2 * row, 2)],
        )
    for row in range(2):
        queries[row] = query_row(attn_in[own + row], projector, ones)
    sends += fetches([(queries, queries_out)], done.at[pl.ds(1 + 2 * near, 1)])
    for copy in sends:
        copy.wait()


def far_kernel(
    rows,
    longitudes,
    bands_count,
    reaches_hbm,
    scales_hbm,
    local,
    lines_hbm,
    cross,
    conv_gain_hbm,
    mixer_hbm,
    attn_gain_hbm,
    projector_hbm,
    final_hbm,
    near_hidden_hbm,
    near_keys,
    near_values,
    near_queries,
    out_hbm,
    reaches,
    scales,
    lines,
    there,
    conv_gain,
    mixer,
    attn_gain,
    projector,
    final,
    raw,
    normed,
    filters,
    bands,
    basis,
    hidden,
    attn_in,
    near_hidden,
    keys,
    values,
    queries,
    bias,
    mixture,
    out,
    sems,
    raw_sems,
    done,
):
    channels = raw.shape[2]
    size = rows * longitudes
    half = longitudes // 2
    position = lax.axis_index("band")
    pole = jnp.logical_or(position == 0, position == bands_count - 1)
    even = 1 - lax.rem(position, 2)
    wide = rows + 2 * PATCH_LAT_EXTENT
    near = 2 * HALO - 2
    far = wide - near
    far_base = (1 - even) * 2
    own_base = even * HALO
    far_slot = (1 - even) * near
    near_slot = even * far
    mine = even * 2
    mine_row = (1 - even) * 2
    copies = fetches(
        [
            (local.at[pl.ds(1 - even, 2)], raw.at[pl.ds(own_base, 2)]),
            (conv_gain_hbm, conv_gain),
            (lines_hbm, lines),
            (cross.at[pl.ds(size, HALO * FILTER_ROWS)], there),
        ],
        sems,
    )

    @pl.when(jnp.logical_not(pole))
    def received():
        fetched = fetches(
            [
                (cross.at[pl.ds(step * longitudes, longitudes)], raw.at[far_base + step])
                for step in range(HALO)
            ],
            raw_sems,
        )
        for copy in fetched:
            copy.wait()

    @pl.when(pole)
    def reflected():
        fetched = fetches(
            [
                (
                    local.at[HALO - 1 - step, pl.ds(side * half, half)],
                    raw.at[far_base + step, pl.ds((1 - side) * half, half)],
                )
                for step in range(HALO)
                for side in range(2)
            ],
            raw_sems,
        )
        for copy in fetched:
            copy.wait()

    copies += fetches(
        [
            (mixer_hbm, mixer),
            (attn_gain_hbm, attn_gain),
            (projector_hbm, projector),
            (near_queries, queries.at[pl.ds(even, 2)]),
            (near_keys, keys.at[pl.ds(near_slot, near)]),
            (near_values, values.at[pl.ds(near_slot, near)]),
            (near_hidden_hbm, near_hidden),
            (final_hbm, final),
            (reaches_hbm, reaches),
            (scales_hbm, scales),
        ],
        sems.at[pl.ds(4, 10)],
    )
    for copy in copies[:4]:
        copy.wait()

    def straight(row):
        return lines[0, row * FILTER_ROWS : (row + 1) * FILTER_ROWS, :].astype(F32)

    def outer(mirror, row):
        flipped = lines[1, mirror * FILTER_ROWS : (mirror + 1) * FILTER_ROWS, :].astype(F32)
        given = there[row * FILTER_ROWS : (row + 1) * FILTER_ROWS, :].astype(F32)
        return jnp.where(pole, flipped, given)

    for u in range(far):
        from_even = straight(0) if u == far - 1 else outer(far - 2 - u, u + 1)
        from_odd = straight(rows - 1) if u == 0 else outer(rows - u, u - 1)
        filters[u] = jnp.where(even > 0, from_even, from_odd)
    norm_rows(far + 2, raw, normed, conv_gain)
    ones = head_ones(channels)
    for row in range(far):
        band_row(row, row, normed, filters, bands.at[row % 2], basis.at[row])
    for copy in copies[4:]:
        copy.wait()
    for row in range(far):
        total = mix_row(raw[row + 1], basis.at[row], mixer)
        hidden[row] = total
        attn_in[row] = scaled_norm(total, attn_gain[...]).astype(BF16)
    for row in range(far):
        slot = far_slot + row
        keys[slot], values[slot] = key_row(attn_in[row], projector, ones)
    queries[mine_row] = query_row(attn_in[mine], projector, ones)
    lanes = HEAD_COUNT * QUERIES
    key_at = lax.broadcasted_iota(jnp.int32, (KEYS, lanes), 0)
    query_at = lax.broadcasted_iota(jnp.int32, (KEYS, lanes), 1) % QUERIES
    distance = jnp.abs(key_at - DISC_REACH - query_at)
    for row in range(rows):
        for a in range(DISC_ROWS):
            bias[row, a * KEYS : (a + 1) * KEYS, :] = jnp.where(
                distance <= reaches[row, a], 0.0, -1e30
            ).astype(F32)
    lane_head = lax.broadcasted_iota(jnp.int32, (1, lanes), 1) // QUERIES
    scale = jnp.zeros((1, lanes), F32)
    for h in range(HEAD_COUNT):
        scale = jnp.where(lane_head == h, scales[h], scale)
    channel_head = lax.broadcasted_iota(jnp.int32, (QUERIES, channels), 1) // HEAD_WIDTH

    def scores_of(row, start):
        probe = queries[row, pl.ds(start, QUERIES), :]
        spread = jnp.concatenate(
            [jnp.where(channel_head == h, probe, jnp.zeros_like(probe)) for h in range(HEAD_COUNT)],
            axis=0,
        )
        nearby = jnp.concatenate(
            [keys[row + a, pl.ds(start, KEYS), :] for a in range(DISC_ROWS)], axis=0
        )
        return lax.dot_general(
            nearby, spread, (((1,), (1,)), ((), ())), preferred_element_type=F32
        )

    def weights_of(row, scores):
        scores = scores + bias[row]
        peak = jnp.max(scores, axis=0, keepdims=True)
        weights = jnp.exp((scores - peak) * scale)
        total = jnp.sum(weights, axis=0, keepdims=True)
        return (weights * (1.0 / total)).astype(BF16)

    def mix(row, start, weights):
        nearby = jnp.concatenate(
            [values[row + a, pl.ds(start, KEYS), :] for a in range(DISC_ROWS)], axis=0
        )
        mixed = lax.dot_general(
            weights, nearby, (((0,), (0,)), ((), ())), preferred_element_type=F32
        )
        result = jnp.zeros((QUERIES, channels), F32)
        for h in range(HEAD_COUNT):
            result = jnp.where(channel_head == h, mixed[h * QUERIES : (h + 1) * QUERIES], result)
        mixture[row, pl.ds(start, QUERIES), :] = result.astype(BF16)

    per_row = longitudes // (QUERIES * UNROLL)

    def attend(step, carry):
        row = step // per_row
        base = (step % per_row) * (QUERIES * UNROLL)
        starts = [pl.multiple_of(base + u * QUERIES, QUERIES) for u in range(UNROLL)]
        scores = [scores_of(row, start) for start in starts]
        weights = [weights_of(row, block) for block in scores]
        for start, block in zip(starts, weights):
            mix(row, start, block)
        return carry

    lax.fori_loop(0, rows * per_row, attend, 0)
    sends = []
    for row in range(rows):
        product = jnp.dot(mixture[row], final[...], preferred_element_type=F32)
        slot = row - even
        far_own = hidden[mine]
        near_own = near_hidden[jnp.clip(slot, 0, 1)]
        own = jnp.where(row == mine_row, far_own, near_own)
        out[row] = (own + product).astype(BF16)
        sends += fetches([(out.at[row], out_hbm.at[row])], done.at[pl.ds(row, 1)])
    for copy in sends:
        copy.wait()


def on_device(
    grid_inputs,
    stencil_prenorm_scale,
    patch_kernel_profiles,
    channel_mixer_tensor,
    softmax_prenorm_scale,
    probe_lookup_content_projector,
    head_logit_scales,
    final_projector,
    azimuth_reaches,
):
    rows, longitudes, channels = grid_inputs.shape
    count = lax.axis_size("band")
    assert rows == HALO and longitudes % (QUERIES * UNROLL) == 0
    assert longitudes % BAND == 0 and channels == 256 and count % 2 == 0
    within = [(i, i ^ 1) for i in range(count)]
    across = [pair for i in range(1, count - 1, 2) for pair in ((i, i + 1), (i + 1, i))]
    size = rows * longitudes
    flat = grid_inputs.reshape(size, channels)
    smem = pl.BlockSpec(memory_space=pltpu.SMEM)
    vmem = pl.BlockSpec(memory_space=pltpu.VMEM)
    hbm = pl.BlockSpec(memory_space=pltpu.HBM)
    limit = pltpu.CompilerParams(vmem_limit_bytes=VMEM_LIMIT)
    lines_shape = (2, rows * FILTER_ROWS, channels)
    payload, lines = pl.pallas_call(
        functools.partial(lines_kernel, rows),
        out_shape=(
            jax.ShapeDtypeStruct((size + rows * FILTER_ROWS, channels), BF16),
            jax.ShapeDtypeStruct(lines_shape, BF16),
        ),
        in_specs=[smem, vmem, hbm],
        out_specs=(hbm, vmem),
        scratch_shapes=[
            pltpu.VMEM((size + rows * FILTER_ROWS, channels), BF16),
            pltpu.VMEM((FILTER_ROWS, channels), F32),
            pltpu.SemaphoreType.DMA((2,)),
        ],
    )(azimuth_reaches, patch_kernel_profiles.transpose(1, 0, 2), flat)
    cross = lax.ppermute(payload, "band", across)
    partner = lax.ppermute(payload, "band", within)
    conv_gain = stencil_prenorm_scale.reshape(1, channels)
    attn_gain = softmax_prenorm_scale.reshape(1, channels)
    near = 2 * HALO - 2
    wide = rows + 2 * PATCH_LAT_EXTENT
    far = wide - near
    padded = longitudes + 2 * DISC_REACH
    sources = [
        pltpu.VMEM(lines_shape, BF16),
        pltpu.VMEM((HALO * FILTER_ROWS, channels), BF16),
        pltpu.VMEM((1, channels), F32),
        pltpu.VMEM(channel_mixer_tensor.shape, BF16),
        pltpu.VMEM((1, channels), F32),
        pltpu.VMEM(probe_lookup_content_projector.shape, BF16),
    ]

    def working(count):
        return [
            pltpu.VMEM((count + 2, longitudes, channels), BF16),
            pltpu.VMEM((count + 2, longitudes + 32, channels), BF16),
            pltpu.VMEM((count + 2, FILTER_ROWS, channels), F32),
            pltpu.VMEM((2, BASIS_COUNT * BAND, channels), BF16),
            pltpu.VMEM((count, longitudes, BASIS_COUNT * channels), BF16),
            pltpu.VMEM((count, longitudes, channels), F32),
            pltpu.VMEM((count, longitudes, channels), BF16),
        ]

    near_state = pl.pallas_call(
        functools.partial(near_kernel, rows, longitudes),
        out_shape=(
            jax.ShapeDtypeStruct((2, longitudes, channels), F32),
            jax.ShapeDtypeStruct((near, padded, channels), BF16),
            jax.ShapeDtypeStruct((near, padded, channels), BF16),
            jax.ShapeDtypeStruct((2, longitudes, channels), BF16),
        ),
        in_specs=[hbm] * 7,
        out_specs=(hbm,) * 4,
        scratch_shapes=sources
        + working(near)
        + [
            pltpu.VMEM((near, padded, channels), BF16),
            pltpu.VMEM((near, padded, channels), BF16),
            pltpu.VMEM((2, longitudes, channels), BF16),
            pltpu.SemaphoreType.DMA((10,)),
            pltpu.SemaphoreType.DMA((2 + 2 * near,)),
        ],
        compiler_params=limit,
        cost_estimate=pl.CostEstimate(flops=8 * 10**9, bytes_accessed=8 * 10**6, transcendentals=0),
    )(
        grid_inputs,
        lines,
        partner,
        conv_gain,
        channel_mixer_tensor,
        attn_gain,
        probe_lookup_content_projector,
    )
    return pl.pallas_call(
        functools.partial(far_kernel, rows, longitudes, count),
        out_shape=jax.ShapeDtypeStruct(grid_inputs.shape, BF16),
        in_specs=[hbm] * 14,
        out_specs=hbm,
        scratch_shapes=[
            pltpu.SMEM(azimuth_reaches.shape, jnp.int32),
            pltpu.SMEM(head_logit_scales.shape, F32),
        ]
        + sources
        + [pltpu.VMEM(final_projector.shape, BF16)]
        + working(far)
        + [
            pltpu.VMEM((2, longitudes, channels), F32),
            pltpu.VMEM((wide, padded, channels), BF16),
            pltpu.VMEM((wide, padded, channels), BF16),
            pltpu.VMEM((rows, longitudes, channels), BF16),
            pltpu.VMEM((rows, DISC_ROWS * KEYS, HEAD_COUNT * QUERIES), F32),
            pltpu.VMEM((rows, longitudes, channels), BF16),
            pltpu.VMEM((rows, longitudes, channels), BF16),
            pltpu.SemaphoreType.DMA((14,)),
            pltpu.SemaphoreType.DMA((2 * HALO,)),
            pltpu.SemaphoreType.DMA((rows,)),
        ],
        compiler_params=limit,
        cost_estimate=pl.CostEstimate(flops=10**10, bytes_accessed=8 * 10**6, transcendentals=10**6),
    )(
        azimuth_reaches,
        head_logit_scales,
        grid_inputs,
        lines,
        cross,
        conv_gain,
        channel_mixer_tensor,
        attn_gain,
        probe_lookup_content_projector,
        final_projector,
        *near_state,
    )


def solution(mesh):
    placed = (
        P(("members", "band"), None, None),
        P(),
        P("band", None, None),
        P(),
        P(),
        P(),
        P(),
        P(),
        P("band", None),
    )
    return jax.shard_map(
        on_device,
        mesh=mesh,
        in_specs=placed,
        out_specs=P(("members", "band"), None, None),
        check_vma=False,
    )
```
